32 devices in a mesh: groups: 2 (over y), lx: 16 (over z, x, core).
Axes of the slice: x: 2, y: 2, z: 4, core: 2. Of those that a mesh axis runs over, the one named last changes fastest.
Arguments:
- syndrome: int32 [32, 2048], P(('groups', 'lx')), parts along dimension 0, may hold values 0 or 1
- events: int32 [32, 2048], P(('groups', 'lx')), parts along dimension 0, may hold values 0 or 1
- boundary: int32 [32, 2048], P(('groups', 'lx')), parts along dimension 0, may hold values from 0 to 3
- syn_table: float32 [2, 256], replicated, may hold values from -3 to 3
- event_table: float32 [2, 256], replicated, may hold values from -3 to 3
- bound_table: float32 [4, 256], replicated, may hold values from -3 to 3
- pos_table: float32 [64, 256], replicated, may hold values from -3 to 3
- norm_attn: float32 [2, 256], replicated, may hold values from 0.1 to 1.9
- w_query: bfloat16 [2, 256, 256], replicated, may hold values from -18 to 18
- w_key: bfloat16 [2, 256, 256], replicated, may hold values from -0.375 to 0.375
- w_value: bfloat16 [2, 256, 256], replicated, may hold values from -0.375 to 0.375
- w_out: bfloat16 [2, 256, 256], replicated, may hold values from -0.75 to 0.75
- norm_mlp: float32 [2, 256], replicated, may hold values from 0.1 to 1.9
- w_up: bfloat16 [2, 256, 1024], replicated, may hold values from -0.375 to 0.375
- w_down: bfloat16 [2, 1024, 256], replicated, may hold values from -0.25 to 0.25
- norm_final: float32 [256], replicated, may hold values from 0.1 to 1.9
- w_read: bfloat16 [256, 2], replicated, may hold values from -0.375 to 0.375
Outputs:
- logits: float32 [2, 32, 2048], P(None, ('groups', 'lx')), parts along dimension 1
The draws below stay inside these ranges and needn't reach their ends.
There are 2 independent parts, one for each index of `groups`. The reference program is written for one: setup_inputs(seed, part) draws one part's arguments, and reference() takes and returns one part's arrays. A program takes and returns all parts, laid end to end along the dimension named above; an argument that names none is the same for every part. Nothing has to cross between parts.
All inputs are finite; a program needn't handle non-finite values. No bound on the sum of `syndrome` or of `events` on one device may be relied on, other than what follows from the above.
Results may differ from the reference program's by a relative error of at most 0.029.
The reference program's roundings to bfloat16 on the way (of `normed`, `weights`, `attended`, `inner` and `final`) count: a program that leaves them out, or rounds other values in their place, can miss the bound.
Values may be sent and summed in bfloat16 or wider, within the bound.
A program may use at most 192 MiB of HBM per device.

```python
import math
import jax
import jax.numpy as jnp
from jax import lax

D = 256
HEADS = 8
FF = 1024
TILE = 64
LAYERS = 2
NXT = 16
NSITE = 2048


def draw_w_query(key, part):
    first = jax.random.fold_in(jax.random.fold_in(key, 11), 0)
    base = jax.random.truncated_normal(first, -4.0, 4.0, (LAYERS, D, D), jnp.float32) * (3.0 / math.sqrt(D))
    return base.astype(jnp.bfloat16)


def touch_ends(result, rng, low, top_value):
    shape = result.shape
    place = [jax.random.randint(jax.random.fold_in(rng, axis), (), 0, shape[axis]) for axis in range(len(shape))]
    result = result.at[tuple(place)].set(low)
    longest = shape.index(max(shape))
    place[longest] = (place[longest] + 1) % shape[longest]
    return result.at[tuple(place)].set(top_value)


def gaussian(stream_key, extent, scale, bound, kind=jnp.bfloat16):
    result = scale * jax.random.normal(stream_key, extent, jnp.float32)
    return jnp.clip(result, min=-bound, max=bound).astype(kind)


def setup_inputs(seed: int = 0, part: int = 0) -> dict:
    splits = jax.random.split(jax.random.key(seed), 18)
    part_keys = jax.random.split(jax.random.fold_in(splits[17], part), 18)
    return {
        "syndrome": touch_ends((jax.random.randint(part_keys[0], (NXT, NSITE), 0, 2) < 1).astype(jnp.int32), jax.random.fold_in(part_keys[0], 1), 0, 1),
        "events": touch_ends((jax.random.randint(part_keys[1], (NXT, NSITE), 0, 4) < 1).astype(jnp.int32), jax.random.fold_in(part_keys[1], 1), 0, 1),
        "boundary": touch_ends(jax.random.randint(part_keys[2], (NXT, NSITE), 0, 4), jax.random.fold_in(part_keys[2], 1), 0, 3).astype(jnp.int32),
        "syn_table": gaussian(splits[3], (2, D), 0.5, 3.0, jnp.float32),
        "event_table": gaussian(splits[4], (2, D), 0.5, 3.0, jnp.float32),
        "bound_table": gaussian(splits[5], (4, D), 0.5, 3.0, jnp.float32),
        "pos_table": gaussian(splits[6], (TILE, D), 0.5, 3.0, jnp.float32),
        "norm_attn": jnp.clip(1.0 + 0.18 * jax.random.normal(splits[7], (LAYERS, D), jnp.float32), 0.1, 1.9),
        "w_query": draw_w_query(jax.random.fold_in(splits[17], 71), part),
        "w_key": gaussian(splits[9], (LAYERS, D, D), D ** -0.5, 0.375),
        "w_value": gaussian(splits[10], (LAYERS, D, D), D ** -0.5, 0.375),
        "w_out": gaussian(splits[11], (LAYERS, D, D), (D // 4) ** -0.5, 0.75),
        "norm_mlp": jnp.clip(1.0 + 0.18 * jax.random.normal(splits[12], (LAYERS, D), jnp.float32), 0.1, 1.9),
        "w_up": gaussian(splits[13], (LAYERS, D, FF), D ** -0.5, 0.375),
        "w_down": gaussian(splits[14], (LAYERS, FF, D), (FF // 2) ** -0.5, 0.25),
        "norm_final": jnp.clip(1.0 + 0.18 * jax.random.normal(splits[15], (D,), jnp.float32), 0.1, 1.9),
        "w_read": gaussian(splits[16], (D, 2), D ** -0.5, 0.375),
    }


def rms_scale(hidden, gain):
    mean_square = lax.optimization_barrier(jnp.mean(hidden * hidden, axis=-1, keepdims=True))
    return hidden * lax.rsqrt(mean_square + 1e-06) * gain

def embed(syndrome, events, boundary, syn_table, event_table, bound_table, pos_table):
    synd_bits = syndrome.astype(jnp.float32)[..., None]
    event_bits = events.astype(jnp.float32)[..., None]
    start = syn_table[0] + synd_bits * (syn_table[1] - syn_table[0])
    start = start + event_table[0] + event_bits * (event_table[1] - event_table[0])
    for kind in range(bound_table.shape[0]):
        chosen = (boundary == kind).astype(jnp.float32)[..., None]
        start = start + chosen * bound_table[kind]
    rows = start.reshape(start.shape[0], -1, pos_table.shape[0], start.shape[-1])
    return rows + pos_table

def attend_row(query_row, key_rows, value_rows, row_valid, dilation, heads):
    tiles, tile_len, width = query_row.shape
    head_dim = width // heads
    padding = ((0, 0), (dilation, dilation), (0, 0), (0, 0))
    key_pad = jnp.pad(key_rows, padding)
    value_pad = jnp.pad(value_rows, padding)

    def one_block(block_index):
        start = block_index * 8
        key_win = lax.dynamic_slice_in_dim(key_pad, start, 8 + 2 * dilation, 1)
        value_win = lax.dynamic_slice_in_dim(value_pad, start, 8 + 2 * dilation, 1)
        query_blk = lax.dynamic_slice_in_dim(query_row, start, 8, 0)
        key_list = []
        value_list = []
        for source in range(3):
            for column in range(3):
                key_list.append(key_win[source, column * dilation:column * dilation + 8])
                value_list.append(value_win[source, column * dilation:column * dilation + 8])
        key_all = jnp.stack(key_list, axis=1).reshape(8, 9 * tile_len, heads, head_dim)
        value_all = jnp.stack(value_list, axis=1).reshape(8, 9 * tile_len, heads, head_dim)
        query_heads = query_blk.reshape(8, tile_len, heads, head_dim)
        scores = jnp.einsum('tqhe,tkhe->thqk', query_heads.astype(jnp.float32), key_all.astype(jnp.float32))
        scores = scores * (1.0 / float(head_dim) ** 0.5)
        tile_cols = start + jnp.arange(8, dtype=jnp.int32)
        col_list = []
        for column in range(3):
            shifted = tile_cols + (column - 1) * dilation
            col_list.append((shifted >= 0) & (shifted < tiles))
        col_valid = jnp.stack(col_list, axis=1)
        valid = row_valid[None, :, None] & col_valid[:, None, :]
        valid = jnp.repeat(valid.reshape(8, 9), tile_len, axis=1)
        scores = jnp.where(valid[:, None, None, :], scores, -1e+30)
        top = lax.optimization_barrier(jnp.max(scores, axis=-1, keepdims=True))
        expd = jnp.exp(scores - top)
        weights = (expd / lax.optimization_barrier(jnp.sum(expd, axis=-1, keepdims=True))).astype(jnp.bfloat16)
        mixed = jnp.einsum('thqk,tkhe->tqhe', weights.astype(jnp.float32), value_all.astype(jnp.float32))
        return mixed.astype(jnp.bfloat16).reshape(8, tile_len, width)
    blocks = lax.map(one_block, jnp.arange(tiles // 8, dtype=jnp.int32))
    return blocks.reshape(tiles, tile_len, width)

def project(inputs, weight):
    flat = inputs.reshape(-1, inputs.shape[-1])
    out = jnp.dot(flat, weight, preferred_element_type=jnp.float32).astype(jnp.bfloat16)
    return out.reshape(inputs.shape[:-1] + (weight.shape[1],))

def reference(syndrome, events, boundary, syn_table, event_table, bound_table, pos_table, norm_attn, w_query, w_key, w_value, w_out, norm_mlp, w_up, w_down, norm_final, w_read):
    stream = embed(syndrome, events, boundary, syn_table, event_table, bound_table, pos_table)
    width = stream.shape[-1]
    row_count = stream.shape[0]
    for layer in range(LAYERS):
        dilation = layer + 1
        normed = rms_scale(stream, norm_attn[layer]).astype(jnp.bfloat16)
        queries = project(normed, w_query[layer])
        keys = project(normed, w_key[layer])
        values = project(normed, w_value[layer])
        padding = ((dilation, dilation), (0, 0), (0, 0), (0, 0))
        key_pad = jnp.pad(keys, padding)
        value_pad = jnp.pad(values, padding)

        def one_row(row_index):
            key_span = lax.dynamic_slice_in_dim(key_pad, row_index, 2 * dilation + 1, 0)
            value_span = lax.dynamic_slice_in_dim(value_pad, row_index, 2 * dilation + 1, 0)
            key_rows = jnp.stack([key_span[0], key_span[dilation], key_span[2 * dilation]])
            value_rows = jnp.stack([value_span[0], value_span[dilation], value_span[2 * dilation]])
            row_valid = jnp.stack([row_index - dilation >= 0, row_index >= 0, row_index + dilation < row_count])
            query_row = lax.dynamic_index_in_dim(queries, row_index, 0, keepdims=False)
            return attend_row(query_row, key_rows, value_rows, row_valid, dilation, HEADS)
        attended = lax.map(one_row, jnp.arange(row_count, dtype=jnp.int32))
        stream = stream + jnp.dot(attended.reshape(-1, width), w_out[layer], preferred_element_type=jnp.float32).reshape(stream.shape)
        normed = rms_scale(stream, norm_mlp[layer]).astype(jnp.bfloat16)
        inner = jax.nn.gelu(jnp.dot(normed.reshape(-1, width), w_up[layer], preferred_element_type=jnp.float32), approximate=True).astype(jnp.bfloat16)
        stream = stream + jnp.dot(inner, w_down[layer], preferred_element_type=jnp.float32).reshape(stream.shape)
    final = rms_scale(stream, norm_final).astype(jnp.bfloat16)
    readout = jnp.dot(final.reshape(-1, width), w_read, preferred_element_type=jnp.float32)
    return readout.reshape(row_count, -1, 2).transpose(2, 0, 1)
```

```python
import functools
import math

import jax
import jax.numpy as jnp
from jax import lax
from jax.experimental import pallas as pl
from jax.experimental.pallas import tpu as pltpu
from jax.sharding import PartitionSpec as P

HEADS = 8
TILE = 64
PAIR = 128
WIDE = 256
COLS = 4
GROUP = 4
GROUPS = HEADS // GROUP
ONES = 16
BF = jnp.bfloat16
F32 = jnp.float32
N_ATTN0, N_ATTN1, N_MLP0, N_MLP1, N_FINAL = range(6, 11)
MESH = pl.DeviceIdType.MESH


def dot(a, b):
    return jnp.dot(a, b, preferred_element_type=F32)


def lanes(parts):
    return jnp.concatenate(parts, axis=1)


def swap(t):
    return lanes([t[:, TILE:], t[:, :TILE]])


def low_mask(rows):
    return lax.broadcasted_iota(jnp.int32, (rows, PAIR), 1) < TILE


def rms(x, gain):
    mean_square = jnp.mean(x * x, axis=0, keepdims=True)
    return x * lax.rsqrt(mean_square + 1e-06) * gain


def gelu(x):
    inner = math.sqrt(2.0 / math.pi) * (x + 0.044715 * (x * x * x))
    return 0.5 * x * (1.0 + jnp.tanh(inner))


def attend(tiles, head_dim):
    scale = math.log2(math.e) / math.sqrt(head_dim)
    half = GROUP * head_dim
    rows = lax.broadcasted_iota(jnp.int32, (half, WIDE), 0) // head_dim
    cols = lax.broadcasted_iota(jnp.int32, (half, WIDE), 1) // TILE
    diag = rows == cols

    def scores(query, keys, _):
        q4 = lanes([query(), query()])
        out = []
        for g in range(GROUPS):
            feats = slice(half * g, half * g + half)
            qg = jnp.where(diag, q4[feats], jnp.zeros((), BF))
            out.append([dot(keys(r, feats), qg) for r in range(3)])
        return out

    def soften(s):
        top = functools.reduce(jnp.maximum, [jnp.max(p, axis=0, keepdims=True) for p in s])
        return [jnp.exp2(((p - top) * scale).astype(BF)) for p in s]

    def mix(exps, values):
        parts = []
        for g in range(GROUPS):
            acc = None
            for r in range(3):
                term = dot(values(r, g), exps[g][r])
                acc = term if acc is None else acc + term
            acc = acc[:half] * (1.0 / acc[half : half + 1])
            parts += [
                acc[head_dim * h : head_dim * h + head_dim, TILE * h : TILE * h + TILE]
                for h in range(GROUP)
            ]
        return jnp.concatenate(parts, axis=0)

    outs = []
    now, before = scores(*tiles[0]), None
    for i in range(len(tiles)):
        later = scores(*tiles[i + 1]) if i + 1 < len(tiles) else None
        exps = [soften(s) for s in now]
        if before is not None:
            outs.append(mix(before, tiles[i - 1][2]))
        now, before = later, exps
    outs.append(mix(before, tiles[-1][2]))
    return lanes(outs).astype(BF)


def feed_forward(stream, gain, wut, wdt):
    normed = rms(stream, gain).astype(BF)
    inner = gelu(dot(wut, normed)).astype(BF)
    return stream + dot(wdt, inner)


def decoder(
    syn_ref, ev_ref, bnd_ref, synt_ref, evt_ref, bt_ref, pos_ref, na_ref,
    wq_ref, wk_ref, wv_ref, wo_ref, nm_ref, wu_ref, wd_ref, nf_ref, wr_ref,
    out_ref,
    tab, base, wqt, wvt, wot, wut, wdt, bit_out, bits, nx, x0, q0, k0, v0, x1, q1, k1, v1,
    log_out, log_in,
    bit_send, bit_recv, side_send, side_recv, vert_send, vert_recv, corner_send, corner_recv,
    log_send, log_recv,
):
    me = lax.axis_index("lx")
    count = lax.axis_size("lx")
    sites = syn_ref.shape[1]
    width = pos_ref.shape[1]
    head_dim = width // HEADS
    half = GROUP * head_dim
    side = sites // (TILE * COLS)
    pairs = side // 2
    bands = count // side
    band = (me // 2) % bands
    col = (me // (2 * bands)) * 2 + me % 2
    row_band, row_place = me // side, me % side

    def device(band, col):
        return (col // 2) * (2 * bands) + band * 2 + col % 2

    def remote(src, dst, send, recv, there):
        return pltpu.make_async_remote_copy(
            src_ref=src, dst_ref=dst, send_sem=send, recv_sem=recv,
            device_id={"lx": there}, device_id_type=MESH,
        )

    barrier = pltpu.get_barrier_semaphore()

    def greet(step, carry):
        pl.semaphore_signal(
            barrier, inc=1, device_id={"lx": (me + step) % count}, device_id_type=MESH
        )
        return carry

    lax.fori_loop(1, count, greet, 0)

    framed = []
    for ref in (syn_ref, ev_ref, bnd_ref):
        row = ref[...].astype(F32)
        framed.append(lanes([row[:, :TILE], row, row[:, sites - TILE :]]))
    for c in range(side):
        picked = [
            row[:, PAIR * (2 * c + j) : PAIR * (2 * c + j + 1)] for row in framed for j in range(3)
        ]
        picked.append(jnp.zeros((7, PAIR), F32))
        bit_out[c] = jnp.concatenate(picked, axis=0).astype(BF)
    pl.semaphore_wait(barrier, count - 1)

    first_row = row_place == 0
    edge_band = jnp.where(first_row, row_band - 1, row_band + 1)
    edge_sends = jnp.logical_or(
        jnp.logical_and(first_row, row_band > 0),
        jnp.logical_and(row_place == side - 1, row_band + 1 < bands),
    )
    targets = [
        (0, True, row_band, row_place + 1),
        (1, edge_sends, edge_band, jnp.where(first_row, side + 1, 0)),
    ]

    def bit_copy(kind, to_band, slot, c):
        return remote(
            bit_out.at[c], bits.at[slot], bit_send.at[kind, c], bit_recv.at[slot],
            device(to_band, c),
        )

    for kind, sends, to_band, slot in targets:
        for c in range(side):
            there = device(to_band, c)

            @pl.when(jnp.logical_and(sends, there != me))
            def _():
                bit_copy(kind, to_band, slot, c).start()

            @pl.when(jnp.logical_and(sends, there == me))
            def _():
                bits[slot] = bit_out[c]

    cols = jnp.concatenate(
        [
            synt_ref[1:2] - synt_ref[0:1], evt_ref[1:2] - evt_ref[0:1], bt_ref[...],
            na_ref[...], nm_ref[...], nf_ref[...], jnp.zeros((5, width), F32),
        ],
        axis=0,
    ).T
    for k in range(tab.shape[0]):
        tab[k] = jnp.broadcast_to(cols[:, k : k + 1], tab.shape[1:])
    start = pos_ref[...] + synt_ref[0:1] + evt_ref[0:1]
    base[...] = jnp.concatenate([start, start], axis=0).T
    for layer in range(2):
        wqt[layer] = wq_ref[layer].T
        wvt[layer] = wv_ref[layer].T
        wot[layer] = wo_ref[layer].T
        wut[layer] = wu_ref[layer].T
        wdt[layer] = wd_ref[layer].T

    left, right = col > 0, col + 1 < side
    above, below = band > 0, band + 1 < bands
    fl_left = jnp.where(left, 1.0, 0.0).astype(F32)
    fl_right = jnp.where(right, 1.0, 0.0).astype(F32)
    lane = lax.broadcasted_iota(jnp.int32, (1, PAIR), 1)
    low = lane < TILE
    one = jnp.ones((1, PAIR), F32)
    low_b = low_mask(width)

    def gain(k, n):
        return lanes([tab[k]] * n)

    def keys_of(n, layer):
        keys = lax.dot_general(
            n, wk_ref[layer], (((0,), (0,)), ((), ())), preferred_element_type=F32
        )
        return keys.astype(BF)


    flags0 = [jnp.where(low, fl_left, 1.0), one, jnp.where(low, 1.0, fl_right)]
    flags0 += [jnp.where(low, 1.0, fl_left), one]

    def embed(row, j):
        x = base[...] + row[j : j + 1] * tab[0] + row[3 + j : 4 + j] * tab[1]
        b = jnp.broadcast_to(row[6 + j : 7 + j], x.shape)
        return x + jnp.where(
            b < 1.5, jnp.where(b < 0.5, tab[2], tab[3]), jnp.where(b < 2.5, tab[4], tab[5])
        )

    def project0(slots, exists, place):
        xs = []
        for slot in slots:
            row = bits[slot].astype(F32)
            xs += [embed(row, j) for j in range(3)]
        x = lanes(xs)
        nf = rms(x, gain(N_ATTN0, 6))
        n = nf.astype(BF)
        keys = keys_of(n, 0)
        v = dot(wvt[0], n)
        for s, slot in enumerate(slots):
            k0[slot] = keys[3 * PAIR * s : 3 * PAIR * (s + 1)]
            vs = [v[:, PAIR * (3 * s + j) : PAIR * (3 * s + j + 1)] for j in range(3)]
            for j in range(3):
                piece = (vs[j] * (flags0[j] * exists[s])).astype(BF)
                for g in range(GROUPS):
                    part = piece[half * g : half * g + half]
                    v0[slot, g, 0:half, PAIR * j : PAIR * j + PAIR] = part
                    if j < 2:
                        v0[slot, g, 0:half, PAIR * (3 + j) : PAIR * (4 + j)] = swap(part)
            for j in range(5):
                flag = jnp.broadcast_to(flags0[j] * exists[s], (ONES, PAIR)).astype(BF)
                for g in range(GROUPS):
                    v0[slot, g, half : half + ONES, PAIR * j : PAIR * j + PAIR] = flag
        if place is not None:
            own = []
            for s in range(2):
                c0, c1, c2 = xs[3 * s : 3 * s + 3]
                x0[place, :, WIDE * s : WIDE * s + PAIR] = jnp.where(low_b, c2, c0)
                x0[place, :, WIDE * s + PAIR : WIDE * s + WIDE] = c1
                n0, n1, n2 = [
                    nf[:, PAIR * (3 * s + j) : PAIR * (3 * s + j + 1)] for j in range(3)
                ]
                own += [jnp.where(low_b, n2, n0), n1]
            q0[place] = dot(wqt[0], lanes(own).astype(BF)).astype(BF)

    def bits_arrive(slot):
        source = band * side + slot - 1

        @pl.when(source != me)
        def _():
            remote(
                bit_out.at[0], bits.at[slot], bit_send.at[0, 0], bit_recv.at[slot], source
            ).wait_recv()

    def own_rows(p, carry):
        bits_arrive(2 * p + 1)
        bits_arrive(2 * p + 2)
        project0((2 * p + 1, 2 * p + 2), (1.0, 1.0), p)
        return carry

    lax.fori_loop(0, pairs, own_rows, 0)
    for slot, there, inner in ((0, above, 1), (side + 1, below, side)):

        @pl.when(there)
        def _():
            bits_arrive(slot)

        @pl.when(jnp.logical_not(there))
        def _():
            bits[slot] = bits[inner]

    project0(
        (0, side + 1),
        (jnp.where(above, 1.0, 0.0).astype(F32), jnp.where(below, 1.0, 0.0).astype(F32)),
        None,
    )

    def queries(ref, p, s):
        out = []
        for j in range(2):
            for want_low in (True, False):

                def query(j=j, want_low=want_low):
                    c = ref[p, :, WIDE * s + PAIR * j : WIDE * s + PAIR * (j + 1)]
                    tile = c[:, :TILE] if want_low else c[:, TILE:]
                    return lanes([tile, tile])

                out.append(query)
        return out

    def window(ref, row, first, second):
        def values(r, g):
            at = row(r) + (g,)
            return lanes(
                [
                    ref[at + (slice(None), slice(PAIR * first, PAIR * first + PAIR))],
                    ref[at + (slice(None), slice(PAIR * second, PAIR * second + TILE))],
                ]
            )

        return values

    def key_tiles(ref, row, tiles):
        def keys(r, feats):
            return jnp.concatenate(
                [ref[row(r) + (slice(TILE * a, TILE * a + TILE * n), feats)] for a, n in tiles], axis=0
            )

        return keys

    plan0 = [
        (((4, 2), (3, 1)), 2, 4), (((0, 3),), 0, 1), (((2, 2), (1, 1)), 1, 3), (((2, 3),), 1, 2),
    ]


    def side_copy(to_right, p):
        mine, theirs = (2, 0) if to_right else (1, 3)
        i = 1 if to_right else 0
        return remote(
            nx.at[mine, p + 1], nx.at[theirs, p + 1], side_send.at[i, p], side_recv.at[i, p],
            device(band, col + 1 if to_right else col - 1),
        )

    def vert_copy(down):
        mine, theirs = (pairs, 0) if down else (1, pairs + 1)
        i = 1 if down else 0
        return remote(
            nx.at[pl.ds(1, 2), mine], nx.at[pl.ds(1, 2), theirs], vert_send.at[i], vert_recv.at[i],
            device(band + 1 if down else band - 1, col),
        )

    def corner_copy(down, to_right):
        mine, theirs = (pairs, 0) if down else (1, pairs + 1)
        mine_c, theirs_c = (2, 0) if to_right else (1, 3)
        i, j = (1 if down else 0), (1 if to_right else 0)
        return remote(
            nx.at[mine_c, mine], nx.at[theirs_c, theirs], corner_send.at[i, j], corner_recv.at[i, j],
            device(band + 1 if down else band - 1, col + 1 if to_right else col - 1),
        )

    def both(a, b):
        return jnp.logical_and(a, b)

    def block0(c, carry):
        p = jnp.where(c == 0, 0, jnp.where(c == 1, pairs - 1, c - 1))
        tiles = []
        for s in range(2):
            row = lambda r, s=s: (2 * p + s + r,)
            for query, (spans, first, second) in zip(queries(q0, p, s), plan0):
                tiles.append((query, key_tiles(k0, row, spans), window(v0, row, first, second)))
        att = attend(tiles, head_dim)
        x = x0[p] + dot(wot[0], att)
        x = feed_forward(x, gain(N_MLP0, 4), wut[0], wdt[0])
        x1[p] = x
        n = rms(x, gain(N_ATTN1, 4))
        for s in range(2):
            a, b = n[:, WIDE * s : WIDE * s + PAIR], n[:, WIDE * s + PAIR : WIDE * s + WIDE]
            nx[1, p + 1, s] = jnp.where(low_b, b, a).astype(BF)
            nx[2, p + 1, s] = jnp.where(low_b, a, b).astype(BF)
        for to_right, there, mine, theirs in ((False, left, 1, 0), (True, right, 2, 3)):

            @pl.when(there)
            def _():
                side_copy(to_right, p).start()

            @pl.when(jnp.logical_not(there))
            def _():
                nx[theirs, p + 1] = nx[mine, p + 1]

        for down, there, at in ((False, above, 0), (True, below, pairs - 1)):

            @pl.when(both(p == at, there))
            def _():
                vert_copy(down).start()

            for to_right, beside in ((False, left), (True, right)):

                @pl.when(both(p == at, both(there, beside)))
                def _():
                    corner_copy(down, to_right).start()

        q1[p] = dot(wqt[1], n.astype(BF)).astype(BF)
        return carry

    lax.fori_loop(0, pairs, block0, 0)

    flags1 = [jnp.where(low, fl_left, 1.0), jnp.where(low, 1.0, fl_right), jnp.where(low, 1.0, fl_left)]

    def project1(e):
        ns = []
        for s in range(2):
            c = [nx[j, e, s] for j in range(4)]
            r = [swap(t) for t in c]
            ns += [jnp.where(low_b, c[0], r[1]), jnp.where(low_b, c[2], r[3])]
            ns += [jnp.where(low_b, r[0], c[1]), jnp.where(low_b, r[2], c[3])]
        n = lanes(ns)
        keys = keys_of(n, 1)
        v = dot(wvt[1], n)
        for s in range(2):
            for sec in range(2):
                at = WIDE * (2 * s + sec)
                k1[e, s, sec] = keys[at : at + WIDE]
                for j in range(2):
                    piece = (v[:, at + PAIR * j : at + PAIR * (j + 1)] * flags1[j]).astype(BF)
                    for g in range(GROUPS):
                        part = piece[half * g : half * g + half]
                        v1[e, s, sec, g, 0:half, PAIR * j : PAIR * j + PAIR] = part
                        if j == 0:
                            v1[e, s, sec, g, 0:half, 2 * PAIR : 3 * PAIR] = swap(part)
                for j in range(3):
                    flag = jnp.broadcast_to(flags1[j], (ONES, PAIR)).astype(BF)
                    for g in range(GROUPS):
                        v1[e, s, sec, g, half : half + ONES, PAIR * j : PAIR * j + PAIR] = flag

    def arrive(k, carry):
        e = jnp.where(k == 0, 1, jnp.where(k == 1, 0, k))
        p = e - 1
        inside = both(p >= 0, p < pairs)
        there = jnp.logical_or(inside, jnp.where(e == 0, above, below))
        for to_right, beside in ((False, right), (True, left)):

            @pl.when(both(inside, beside))
            def _():
                side_copy(to_right, p).wait_recv()

        for down, from_there, at in ((True, above, 0), (False, below, pairs + 1)):

            @pl.when(both(e == at, from_there))
            def _():
                vert_copy(down).wait_recv()
                for to_right, beside, mine, theirs in ((False, right, 2, 3), (True, left, 1, 0)):

                    @pl.when(beside)
                    def _():
                        corner_copy(down, to_right).wait_recv()

                    @pl.when(jnp.logical_not(beside))
                    def _():
                        nx[theirs, at] = nx[mine, at]

            @pl.when(both(e == at, jnp.logical_not(from_there)))
            def _():
                k1[at] = k1[1 if at == 0 else pairs]
                v1[at] = jnp.zeros(v1.shape[1:], BF)

        @pl.when(there)
        def _():
            project1(e)

        return carry

    plan1 = [
        (0, ((2, 2), (1, 1)), 1, 2), (1, ((0, 3),), 0, 1),
        (0, ((0, 3),), 0, 1), (1, ((2, 2), (1, 1)), 1, 2),
    ]

    def log_copy(p, s):
        i = 2 * p + s
        return remote(
            log_out.at[i], log_in.at[col], log_send.at[i], log_recv.at[col], band * side + i
        )

    def block1(p, carry):
        lax.fori_loop(jnp.where(p == 0, 0, p + 2), p + 3, arrive, 0)
        tiles = []
        for s in range(2):
            for query, (sec, spans, first, second) in zip(queries(q1, p, s), plan1):
                row = lambda r, s=s, sec=sec: (p + r, s, sec)
                tiles.append((query, key_tiles(k1, row, spans), window(v1, row, first, second)))
        att = attend(tiles, head_dim)
        x = x1[p] + dot(wot[1], att)
        x = feed_forward(x, gain(N_MLP1, 4), wut[1], wdt[1])
        n = rms(x, gain(N_FINAL, 4)).astype(BF)
        logit = dot(wr_ref[...], n)
        outs = logit.shape[0]
        for s in range(2):
            t3, t0, t1, t2 = [
                logit[:, WIDE * s + TILE * t : WIDE * s + TILE * (t + 1)] for t in range(4)
            ]
            rows = [lanes([t0, t1]), lanes([t2, t3])]
            log_out[2 * p + s] = jnp.concatenate(
                rows + [jnp.zeros((8 - 2 * outs, PAIR), F32)], axis=0
            )
            to = band * side + 2 * p + s

            @pl.when(to != me)
            def _():
                log_copy(p, s).start()

            @pl.when(to == me)
            def _():
                log_in[col] = log_out[2 * p + s]

        return carry

    lax.fori_loop(0, pairs, block1, 0)

    for c in range(side):
        source = device(row_band, c)

        @pl.when(source != me)
        def _():
            remote(
                log_out.at[0], log_in.at[c], log_send.at[0], log_recv.at[c], source
            ).wait_recv()

    outs = out_ref.shape[0]
    pieces = []
    for c in range(side):
        got = log_in[c]
        pieces += [got[0:outs], got[outs : 2 * outs]]
    out_ref[...] = lanes(pieces)

    for kind, sends, to_band, slot in targets:
        for c in range(side):
            there = device(to_band, c)

            @pl.when(jnp.logical_and(sends, there != me))
            def _():
                bit_copy(kind, to_band, slot, c).wait_send()

    for to_right, beside in ((False, left), (True, right)):

        @pl.when(beside)
        def _():
            def sent(p, carry):
                side_copy(to_right, p).wait_send()
                return carry

            lax.fori_loop(0, pairs, sent, 0)

    for down, there in ((False, above), (True, below)):

        @pl.when(there)
        def _():
            vert_copy(down).wait_send()
            for to_right, beside in ((False, left), (True, right)):

                @pl.when(beside)
                def _():
                    corner_copy(down, to_right).wait_send()

    def log_sent(p, carry):
        for s in range(2):

            @pl.when(band * side + 2 * p + s != me)
            def _():
                log_copy(p, s).wait_send()

        return carry

    lax.fori_loop(0, pairs, log_sent, 0)


def on_device(
    syndrome, events, boundary, syn_table, event_table, bound_table, pos_table, norm_attn,
    w_query, w_key, w_value, w_out, norm_mlp, w_up, w_down, norm_final, w_read,
):
    sites = syndrome.shape[1]
    width = pos_table.shape[1]
    ff = w_up.shape[2]
    side = sites // (TILE * COLS)
    pairs = side // 2
    half = width // GROUPS
    vmem = pl.BlockSpec(memory_space=pltpu.VMEM)
    dma = pltpu.SemaphoreType.DMA
    outs = w_read.shape[1]
    logits = pl.pallas_call(
        decoder,
        name="decoder",
        out_shape=jax.ShapeDtypeStruct((outs, sites), F32),
        in_specs=[vmem] * 17,
        out_specs=vmem,
        scratch_shapes=[
            pltpu.VMEM((11, width, PAIR), F32),
            pltpu.VMEM((width, PAIR), F32),
            pltpu.VMEM((2, width, width), BF),
            pltpu.VMEM((2, width, width), BF),
            pltpu.VMEM((2, width, width), BF),
            pltpu.VMEM((2, ff, width), BF),
            pltpu.VMEM((2, width, ff), BF),
            pltpu.VMEM((side, 16, PAIR), BF),
            pltpu.VMEM((side + 2, 16, PAIR), BF),
            pltpu.VMEM((4, pairs + 2, 2, width, PAIR), BF),
            pltpu.VMEM((pairs, width, 2 * WIDE), F32),
            pltpu.VMEM((pairs, width, 2 * WIDE), BF),
            pltpu.VMEM((side + 2, 3 * PAIR, width), BF),
            pltpu.VMEM((side + 2, GROUPS, half + ONES, 5 * PAIR), BF),
            pltpu.VMEM((pairs, width, 2 * WIDE), F32),
            pltpu.VMEM((pairs, width, 2 * WIDE), BF),
            pltpu.VMEM((pairs + 2, 2, 2, WIDE, width), BF),
            pltpu.VMEM((pairs + 2, 2, 2, GROUPS, half + ONES, 3 * PAIR), BF),
            pltpu.VMEM((side, 8, PAIR), F32),
            pltpu.VMEM((side, 8, PAIR), F32),
            dma((2, side)),
            dma((side + 2,)),
            dma((2, pairs)),
            dma((2, pairs)),
            dma((2,)),
            dma((2,)),
            dma((2, 2)),
            dma((2, 2)),
            dma((side,)),
            dma((side,)),
        ],
        compiler_params=pltpu.CompilerParams(
            vmem_limit_bytes=56 * 1024 * 1024, collective_id=0, has_side_effects=True
        ),
    )(
        syndrome, events, boundary, syn_table, event_table, bound_table, pos_table, norm_attn,
        w_query, w_key, w_value, w_out, norm_mlp, w_up, w_down, norm_final[None], w_read.T,
    )
    return logits[:, None, :]


def solution(mesh):
    rows = P(("groups", "lx"), None)
    return jax.shard_map(
        on_device,
        mesh=mesh,
        in_specs=(rows,) * 3 + (P(),) * 14,
        out_specs=P(None, ("groups", "lx"), None),
        check_vma=False,
    )
```

```python
import functools
import math

import jax
import jax.numpy as jnp
from jax import lax
from jax.experimental import pallas as pl
from jax.experimental.pallas import tpu as pltpu
from jax.sharding import PartitionSpec as P

HEADS = 8
TILE = 64
PAIR = 128
WIDE = 256
COLS = 4
GROUP = 2
GROUPS = HEADS // GROUP
ONES = 16
BF = jnp.bfloat16
F32 = jnp.float32
LEAD = 2
KINDS = 16
N_ATTN0, N_ATTN1, N_MLP0, N_MLP1, N_FINAL = range(5)
MESH = pl.DeviceIdType.MESH


def dot(a, b):
    return jnp.dot(a, b, preferred_element_type=F32)


def lanes(parts):
    return jnp.concatenate(parts, axis=1)


def swap(t):
    return lanes([t[:, TILE:], t[:, :TILE]])


def low_mask(rows):
    return lax.broadcasted_iota(jnp.int32, (rows, PAIR), 1) < TILE


def rms(x, gain):
    mean_square = jnp.mean(x * x, axis=0, keepdims=True)
    return x * lax.rsqrt(mean_square + 1e-06) * gain


def gelu(x):
    first = math.sqrt(2.0 / math.pi)
    return x + x * jnp.tanh(x * (first + (first * 0.044715) * (x * x)))


def attend(pairs, head_dim, first_low):
    chunk = PAIR
    low = low_mask(chunk)
    low_wide = lanes([low_mask(TILE)] * 2)
    in_a = low_wide if first_low else jnp.logical_not(low_wide)
    zero = jnp.zeros((), BF)

    def prepare(query, keys, _, g):
        feats = slice(chunk * (g // 2), chunk * (g // 2) + chunk)
        q = query()[feats]
        at = 2 * head_dim * (g % 2)
        none = jnp.zeros((head_dim, PAIR), BF)

        def block(t):
            rows = []
            for h in range(chunk // head_dim):
                part = t[head_dim * h : head_dim * h + head_dim]
                if h == 2 * (g % 2):
                    rows.append(lanes([part, none]))
                elif h == 2 * (g % 2) + 1:
                    rows.append(lanes([none, part]))
                else:
                    rows.append(lanes([none, none]))
            return jnp.concatenate(rows, axis=0)

        q_low, q_high = jnp.where(low, q, zero), jnp.where(low, zero, q)
        q_a, q_b = (q_low, q_high) if first_low else (q_high, q_low)
        shared = block(q)
        apart = jnp.concatenate([block(q_a), block(q_b)], axis=0)
        return keys, feats, shared, apart

    def scores(ready, r):
        keys, feats, shared, apart = ready
        k = keys(r, feats)
        parts = [
            dot(k[TILE : 3 * TILE], shared), dot(lanes([k[:TILE], k[3 * TILE :]]), apart),
        ]
        top = functools.reduce(
            jnp.maximum, [jnp.max(p.reshape(-1, 8, WIDE), axis=0) for p in parts]
        )
        return parts, top

    def soften(parts, top):
        return [jnp.exp2((p - top).astype(BF)) for p in parts]

    def mix(acc, exps, values, g, r):
        shared, apart = exps
        e = jnp.concatenate(
            [jnp.where(in_a, apart, zero), shared, jnp.where(in_a, zero, apart)], axis=0
        )
        term = dot(values(r, g), e)
        return term if acc is None else acc + term

    def finish(acc):
        acc = acc[: 2 * head_dim] * (1.0 / acc[2 * head_dim : 2 * head_dim + 1])
        return jnp.concatenate([acc[:head_dim, :PAIR], acc[head_dim:, PAIR:]], axis=0)

    units = [(pair, g) for pair in pairs for g in range(GROUPS)]
    done, raw, soft = [], {}, {}
    for i in range(-LEAD, len(units) + 1):
        ahead, now, back = i + LEAD, i, i - 1
        if ahead < len(units):
            ready = prepare(*units[ahead][0], units[ahead][1])
            raw[ahead] = []
        if 0 <= now < len(units):
            top = functools.reduce(jnp.maximum, [t for _, t in raw[now]])
            top = jnp.max(top, axis=0, keepdims=True)
            soft[now] = []
        acc = None
        for r in range(3):
            if ahead < len(units):
                raw[ahead].append(scores(ready, r))
            if 0 <= now < len(units):
                soft[now].append(soften(raw[now][r][0], top))
            if 0 <= back < len(units):
                acc = mix(acc, soft[back][r], units[back][0][2], units[back][1], r)
        if 0 <= back < len(units):
            done.append(finish(acc))
    n = GROUPS
    return lanes(
        [jnp.concatenate(done[n * i : n * i + n], axis=0) for i in range(len(pairs))]
    ).astype(BF)


def feed_forward(stream, gain, wut, wdt):
    normed = rms(stream, gain).astype(BF)
    inner = gelu(dot(wut, normed)).astype(BF)
    return stream + dot(wdt, inner)


def decoder(
    syn_hbm, ev_hbm, bnd_hbm, synt_hbm, evt_hbm, bt_hbm, pos_hbm, na_hbm,
    wq_hbm, wk_hbm, wv_hbm, wo_hbm, nm_hbm, wu_hbm, wd_hbm, nf_hbm, wr_hbm,
    out_ref,
    syn_ref, ev_ref, bnd_ref, synt_ref, evt_ref, bt_ref, pos_ref, na_ref,
    wq_ref, wk_ref, wv_ref, wo_ref, nm_ref, wu_ref, wd_ref, nf_ref, wr_ref,
    load_sem, layer_sem,
    tab, table, hot, wqt, wvt, wot, wut, wdt, bit_out, bits, nx, x0, q0, k0, v0, x1, q1, k1, v1,
    log_out,
    bit_send, bit_recv, side_send, side_recv, vert_send, vert_recv, corner_send, corner_recv,
    log_send, log_recv, log_own,
):
    me = lax.axis_index("lx")
    count = lax.axis_size("lx")
    sites = syn_ref.shape[1]
    width = pos_ref.shape[1]
    head_dim = width // HEADS
    part = GROUP * head_dim
    side = sites // (TILE * COLS)
    pairs = side // 2
    bands = count // side
    band = (me // 2) % bands
    col = (me // (2 * bands)) * 2 + me % 2
    row_band, row_place = me // side, me % side

    def device(band, col):
        return (col // 2) * (2 * bands) + band * 2 + col % 2

    def remote(src, dst, send, recv, there):
        return pltpu.make_async_remote_copy(
            src_ref=src, dst_ref=dst, send_sem=send, recv_sem=recv,
            device_id={"lx": there}, device_id_type=MESH,
        )

    def whole(i, src, dst):
        return pltpu.make_async_copy(src, dst, load_sem.at[i])

    def by_layer(i, layer, src, dst):
        return pltpu.make_async_copy(src.at[layer], dst.at[layer], layer_sem.at[i, layer])

    bit_loads = [
        whole(i, *refs)
        for i, refs in enumerate([(syn_hbm, syn_ref), (ev_hbm, ev_ref), (bnd_hbm, bnd_ref)])
    ]
    small_loads = [
        whole(3 + i, *refs)
        for i, refs in enumerate(
            [
                (synt_hbm, synt_ref), (evt_hbm, evt_ref), (bt_hbm, bt_ref), (pos_hbm, pos_ref),
                (na_hbm, na_ref), (nm_hbm, nm_ref), (nf_hbm, nf_ref), (wr_hbm, wr_ref),
            ]
        )
    ]
    stacks = [
        (wq_hbm, wq_ref), (wk_hbm, wk_ref), (wv_hbm, wv_ref), (wo_hbm, wo_ref), (wu_hbm, wu_ref),
        (wd_hbm, wd_ref),
    ]
    weight_loads = [
        [by_layer(i, layer, *refs) for i, refs in enumerate(stacks)] for layer in range(2)
    ]
    for load in bit_loads:
        load.start()

    barrier = pltpu.get_barrier_semaphore()

    def greet(step, carry):
        pl.semaphore_signal(
            barrier, inc=1, device_id={"lx": (me + step) % count}, device_id_type=MESH
        )
        return carry

    lax.fori_loop(1, count, greet, 0)
    for load in weight_loads[0][:3] + small_loads + weight_loads[0][3:] + weight_loads[1]:
        load.start()
    for load in bit_loads:
        load.wait()

    framed = []
    for ref in (syn_ref, ev_ref, bnd_ref):
        row = ref[...].astype(F32)
        framed.append(lanes([row[:, :TILE], row, row[:, sites - TILE :]]))
    for c in range(side):
        picked = [
            row[:, PAIR * (2 * c + j) : PAIR * (2 * c + j + 1)] for row in framed for j in range(3)
        ]
        picked.append(jnp.zeros((7, PAIR), F32))
        bit_out[c] = jnp.concatenate(picked, axis=0).astype(BF)
    pl.semaphore_wait(barrier, count - 1)

    first_row = row_place == 0
    edge_band = jnp.where(first_row, row_band - 1, row_band + 1)
    edge_sends = jnp.logical_or(
        jnp.logical_and(first_row, row_band > 0),
        jnp.logical_and(row_place == side - 1, row_band + 1 < bands),
    )
    targets = [
        (0, True, row_band, row_place + 1),
        (1, edge_sends, edge_band, jnp.where(first_row, side + 1, 0)),
    ]

    def bit_copy(kind, to_band, slot, c):
        return remote(
            bit_out.at[c], bits.at[slot], bit_send.at[kind, c], bit_recv.at[slot],
            device(to_band, c),
        )

    for kind, sends, to_band, slot in targets:
        for c in range(side):
            there = device(to_band, c)

            @pl.when(jnp.logical_and(sends, there != me))
            def _():
                bit_copy(kind, to_band, slot, c).start()

            @pl.when(jnp.logical_and(sends, there == me))
            def _():
                bits[slot] = bit_out[c]

    for load in small_loads:
        load.wait()
    cols = jnp.concatenate(
        [na_ref[...], nm_ref[...], nf_ref[...], jnp.zeros((3, width), F32)], axis=0
    ).T
    for k in range(tab.shape[0]):
        tab[k] = jnp.broadcast_to(cols[:, k : k + 1], tab.shape[1:])
    rest = jnp.concatenate(
        [
            pos_ref[...] + synt_ref[0:1] + evt_ref[0:1],
            synt_ref[1:2] - synt_ref[0:1], evt_ref[1:2] - evt_ref[0:1], bt_ref[...],
            jnp.zeros((KINDS - 2 - bt_ref.shape[0], width), F32),
        ],
        axis=0,
    )
    pieces = []
    for _ in range(3):
        piece = rest.astype(BF)
        pieces.append(piece)
        rest = rest - piece.astype(F32)
    used = 3 * (TILE + KINDS)
    pieces.append(jnp.zeros((table.shape[1] - used, width), BF))
    table[...] = jnp.concatenate(pieces, axis=0).T
    place_of = lax.broadcasted_iota(jnp.int32, (TILE, PAIR), 1) % TILE
    hot[...] = jnp.where(
        place_of == lax.broadcasted_iota(jnp.int32, (TILE, PAIR), 0), 1.0, 0.0
    ).astype(BF)
    for load in weight_loads[0][:3]:
        load.wait()
    wqt[0] = wq_ref[0].T
    wvt[0] = wv_ref[0].T

    def turn(p):
        layer, side_of = p // 2, p % 2
        w, f = width // 2, wu_ref.shape[2] // 2
        at_w, at_f = pl.multiple_of(side_of * w, w), pl.multiple_of(side_of * f, f)
        wot[layer, pl.ds(at_w, w), :] = wo_ref[layer, :, pl.ds(at_w, w)].T
        wut[layer, pl.ds(at_f, f), :] = wu_ref[layer, :, pl.ds(at_f, f)].T
        wdt[layer, :, pl.ds(at_f, f)] = (
            wd_ref[layer, pl.ds(at_f, f), :] * jnp.asarray(0.5, BF)
        ).T

    left, right = col > 0, col + 1 < side
    above, below = band > 0, band + 1 < bands

    def mirror(i, last):
        return jnp.where(below, i, last - i)

    fl_left = jnp.where(left, 1.0, 0.0).astype(F32)
    fl_right = jnp.where(right, 1.0, 0.0).astype(F32)
    lane = lax.broadcasted_iota(jnp.int32, (1, PAIR), 1)
    low = lane < TILE
    one = jnp.ones((1, PAIR), F32)
    low_b = low_mask(width)

    def gain(k, n):
        return lanes([tab[k]] * n)

    def keys_of(n, layer):
        keys = lax.dot_general(
            n, wk_ref[layer], (((0,), (0,)), ((), ())), preferred_element_type=F32
        )
        return keys.astype(BF)

    scale = math.log2(math.e) / math.sqrt(head_dim)

    def put_values(ref, at, v, flag, lane):
        piece = (v * flag).astype(BF)
        ones = jnp.broadcast_to(flag, (ONES, PAIR)).astype(BF)
        for g in range(GROUPS):
            ref[at + (g, slice(0, part), slice(lane, lane + PAIR))] = piece[
                part * g : part * g + part
            ]
            ref[at + (g, slice(part, part + ONES), slice(lane, lane + PAIR))] = ones


    flags0 = [jnp.where(low, fl_left, 1.0), one, jnp.where(low, 1.0, fl_right)]
    kind = lax.broadcasted_iota(jnp.int32, (KINDS, PAIR), 0).astype(F32)

    def one_hot(row, j):
        chosen = jnp.where(row[6 + j : 7 + j] == kind - 2.0, 1.0, 0.0)
        marks = jnp.where(
            kind == 0.0, row[j : j + 1], jnp.where(kind == 1.0, row[3 + j : 4 + j], chosen)
        ).astype(BF)
        spare = jnp.zeros((table.shape[1] - 3 * (TILE + KINDS), PAIR), BF)
        return jnp.concatenate([hot[...], marks] * 3 + [spare], axis=0)

    def project0(slots, exists, place):
        marks = []
        for slot in slots:
            row = bits[slot].astype(F32)
            marks += [one_hot(row, j) for j in range(3)]
        x = dot(table[...], lanes(marks))
        n = rms(x, gain(N_ATTN0, 6)).astype(BF)
        keys = keys_of(n, 0)
        v = dot(wvt[0], n)
        for s, slot in enumerate(slots):
            k0[slot] = keys[3 * PAIR * s : 3 * PAIR * (s + 1)]
            for j in range(3):
                at = PAIR * (3 * s + j)
                put_values(v0, (slot,), v[:, at : at + PAIR], flags0[j] * exists[s], PAIR * j)
        if place is not None:
            own = []
            for s in range(2):
                c = [x[:, PAIR * (3 * s + j) : PAIR * (3 * s + j + 1)] for j in range(3)]
                x0[place, :, WIDE * s : WIDE * s + PAIR] = jnp.where(low_b, c[1], c[0])
                x0[place, :, WIDE * s + PAIR : WIDE * s + WIDE] = jnp.where(low_b, c[2], c[1])
                c = [n[:, PAIR * (3 * s + j) : PAIR * (3 * s + j + 1)] for j in range(3)]
                own += [jnp.where(low_b, c[1], c[0]), jnp.where(low_b, c[2], c[1])]
            q0[place] = (dot(wqt[0], lanes(own)) * scale).astype(BF)

    def bits_arrive(slot):
        source = band * side + slot - 1

        @pl.when(source != me)
        def _():
            remote(
                bit_out.at[0], bits.at[slot], bit_send.at[0, 0], bit_recv.at[slot], source
            ).wait_recv()

    def own_rows(p, carry):
        bits_arrive(2 * p + 1)
        bits_arrive(2 * p + 2)
        for at, loads in ((0, weight_loads[0][3:]), (2, weight_loads[1])):

            @pl.when(p == at)
            def _():
                for load in loads:
                    load.wait()

        turn(p)
        project0((2 * p + 1, 2 * p + 2), (1.0, 1.0), p)
        return carry

    lax.fori_loop(0, pairs, own_rows, 0)
    for slot, there, inner in ((0, above, 1), (side + 1, below, side)):

        @pl.when(there)
        def _():
            bits_arrive(slot)

        @pl.when(jnp.logical_not(there))
        def _():
            bits[slot] = bits[inner]

    wqt[1] = wq_ref[1].T
    wvt[1] = wv_ref[1].T
    project0(
        (0, side + 1),
        (jnp.where(above, 1.0, 0.0).astype(F32), jnp.where(below, 1.0, 0.0).astype(F32)),
        None,
    )

    def query_pair(ref, p, s, j):
        return lambda: ref[p, :, WIDE * s + PAIR * j : WIDE * s + PAIR * (j + 1)]


    def side_copy(to_right, p):
        mine, theirs = (2, 0) if to_right else (1, 3)
        i = 1 if to_right else 0
        return remote(
            nx.at[mine, p + 1], nx.at[theirs, p + 1], side_send.at[i, p], side_recv.at[i, p],
            device(band, col + 1 if to_right else col - 1),
        )

    def vert_copy(down):
        mine, theirs = (pairs, 0) if down else (1, pairs + 1)
        i = 1 if down else 0
        return remote(
            nx.at[pl.ds(1, 2), mine], nx.at[pl.ds(1, 2), theirs], vert_send.at[i], vert_recv.at[i],
            device(band + 1 if down else band - 1, col),
        )

    def corner_copy(down, to_right):
        mine, theirs = (pairs, 0) if down else (1, pairs + 1)
        mine_c, theirs_c = (2, 0) if to_right else (1, 3)
        i, j = (1 if down else 0), (1 if to_right else 0)
        return remote(
            nx.at[mine_c, mine], nx.at[theirs_c, theirs], corner_send.at[i, j], corner_recv.at[i, j],
            device(band + 1 if down else band - 1, col + 1 if to_right else col - 1),
        )

    def both(a, b):
        return jnp.logical_and(a, b)

    def block0(c, carry):
        p = mirror(jnp.where(c == 0, pairs - 1, c - 1), pairs - 1)
        work = []
        for s in range(2):
            for j in range(2):

                def keys(r, feats, s=s, j=j):
                    return k0[2 * p + s + r, PAIR * j : PAIR * j + WIDE, feats]

                def values(r, g, s=s, j=j):
                    return v0[2 * p + s + r, g, :, PAIR * j : PAIR * j + WIDE]

                work.append((query_pair(q0, p, s, j), keys, values))
        att = attend(work, head_dim, False)
        x = x0[p] + dot(wot[0], att)
        x = feed_forward(x, gain(N_MLP0, 4), wut[0], wdt[0])
        n = rms(x, gain(N_ATTN1, 4)).astype(BF)

        def regroup(t):
            out = []
            for s in range(2):
                a, b = t[:, WIDE * s : WIDE * s + PAIR], t[:, WIDE * s + PAIR : WIDE * s + WIDE]
                out += [jnp.where(low_b, a, swap(b)), jnp.where(low_b, swap(a), b)]
            return lanes(out)

        x1[p] = regroup(x)
        for s in range(2):
            for j in range(2):
                nx[1 + j, p + 1, s] = n[:, WIDE * s + PAIR * j : WIDE * s + PAIR * (j + 1)]
        for to_right, there, mine, theirs in ((False, left, 1, 0), (True, right, 2, 3)):

            @pl.when(there)
            def _():
                side_copy(to_right, p).start()

            @pl.when(jnp.logical_not(there))
            def _():
                nx[theirs, p + 1] = nx[mine, p + 1]

        for down, there, at in ((False, above, 0), (True, below, pairs - 1)):

            @pl.when(both(p == at, there))
            def _():
                vert_copy(down).start()

            for to_right, beside in ((False, left), (True, right)):

                @pl.when(both(p == at, both(there, beside)))
                def _():
                    corner_copy(down, to_right).start()

        q1[p] = (dot(wqt[1], regroup(n)) * scale).astype(BF)
        return carry

    lax.fori_loop(0, pairs, block0, 0)

    flags1 = [jnp.where(low, fl_left, 1.0), jnp.where(low, 1.0, fl_right)]

    def project1(e):
        ns = []
        for s in range(2):
            c = [nx[j, e, s] for j in range(4)]
            r = [swap(t) for t in c]
            ns += [jnp.where(low_b, c[0], r[1]), jnp.where(low_b, c[2], r[3])]
            ns += [jnp.where(low_b, r[0], c[1]), jnp.where(low_b, r[2], c[3])]
        n = lanes(ns)
        v = dot(wvt[1], n)
        keys = keys_of(n, 1)
        for s in range(2):
            for sec in range(2):
                at = WIDE * (2 * s + sec)
                k1[e, s, sec] = keys[at : at + WIDE]
                for j in range(2):
                    put_values(
                        v1, (e, s, sec), v[:, at + PAIR * j : at + PAIR * (j + 1)], flags1[j],
                        PAIR * j,
                    )

    def arrive(k, carry):
        e = mirror(jnp.where(k == 0, 1, jnp.where(k == 1, 0, k)), pairs + 1)
        p = e - 1
        inside = both(p >= 0, p < pairs)
        there = jnp.logical_or(inside, jnp.where(e == 0, above, below))
        for to_right, beside in ((False, right), (True, left)):

            @pl.when(both(inside, beside))
            def _():
                side_copy(to_right, p).wait_recv()

        for down, from_there, at in ((True, above, 0), (False, below, pairs + 1)):

            @pl.when(both(e == at, from_there))
            def _():
                vert_copy(down).wait_recv()
                for to_right, beside, mine, theirs in ((False, right, 2, 3), (True, left, 1, 0)):

                    @pl.when(beside)
                    def _():
                        corner_copy(down, to_right).wait_recv()

                    @pl.when(jnp.logical_not(beside))
                    def _():
                        nx[theirs, at] = nx[mine, at]

            @pl.when(both(e == at, jnp.logical_not(from_there)))
            def _():
                k1[at] = k1[1 if at == 0 else pairs]
                v1[at] = jnp.zeros(v1.shape[1:], BF)

        @pl.when(there)
        def _():
            project1(e)

        return carry

    def log_copy(p, s):
        i = 2 * p + s
        return remote(
            log_out.at[i], log_place(col), log_send.at[i], log_recv.at[col], band * side + i
        )

    def log_place(c):
        return out_ref.at[:, :, pl.ds(pl.multiple_of(c * WIDE, WIDE), WIDE)]

    def log_stay(i):
        return pltpu.make_async_copy(log_out.at[i], log_place(col), log_own)

    def block1(c, carry):
        near_end = c >= pairs - 2
        p = mirror(jnp.where(near_end, 2 * pairs - 3 - c, c), pairs - 1)
        begin = jnp.where(c == 0, 0, jnp.where(c == pairs - 1, pairs + 2, c + 2))
        lax.fori_loop(begin, jnp.where(near_end, pairs + 2, c + 3), arrive, 0)
        work = []
        for s in range(2):
            for sec in range(2):

                def keys(r, feats, s=s, sec=sec):
                    return k1[p + r, s, sec, :, feats]

                def values(r, g, s=s, sec=sec):
                    return v1[p + r, s, sec, g]

                work.append((query_pair(q1, p, s, sec), keys, values))
        att = attend(work, head_dim, True)
        x = x1[p] + dot(wot[1], att)
        x = feed_forward(x, gain(N_MLP1, 4), wut[1], wdt[1])
        n = rms(x, gain(N_FINAL, 4)).astype(BF)
        logit = dot(wr_ref[...], n)
        for s in range(2):
            t1, t3, t0, t2 = [
                logit[:, WIDE * s + TILE * t : WIDE * s + TILE * (t + 1)] for t in range(4)
            ]
            row = lanes([t0, t1, t2, t3])
            for k in range(row.shape[0]):
                log_out[2 * p + s, k] = row[k : k + 1]
            to = band * side + 2 * p + s

            @pl.when(to != me)
            def _():
                log_copy(p, s).start()

            @pl.when(to == me)
            def _():
                log_stay(2 * p + s).start()

        return carry

    lax.fori_loop(0, pairs, block1, 0)

    for c in range(side):
        source = device(row_band, c)

        @pl.when(source != me)
        def _():
            remote(
                log_out.at[0], log_place(c), log_send.at[0], log_recv.at[c], source
            ).wait_recv()

    for kind, sends, to_band, slot in targets:
        for c in range(side):
            there = device(to_band, c)

            @pl.when(jnp.logical_and(sends, there != me))
            def _():
                bit_copy(kind, to_band, slot, c).wait_send()

    for to_right, beside in ((False, left), (True, right)):

        @pl.when(beside)
        def _():
            def sent(p, carry):
                side_copy(to_right, p).wait_send()
                return carry

            lax.fori_loop(0, pairs, sent, 0)

    for down, there in ((False, above), (True, below)):

        @pl.when(there)
        def _():
            vert_copy(down).wait_send()
            for to_right, beside in ((False, left), (True, right)):

                @pl.when(beside)
                def _():
                    corner_copy(down, to_right).wait_send()

    def log_sent(p, carry):
        for s in range(2):

            @pl.when(band * side + 2 * p + s != me)
            def _():
                log_copy(p, s).wait_send()

        return carry

    lax.fori_loop(0, pairs, log_sent, 0)

    @pl.when(row_band == band)
    def _():
        log_stay(row_place).wait()


def on_device(
    syndrome, events, boundary, syn_table, event_table, bound_table, pos_table, norm_attn,
    w_query, w_key, w_value, w_out, norm_mlp, w_up, w_down, norm_final, w_read,
):
    sites = syndrome.shape[1]
    width = pos_table.shape[1]
    ff = w_up.shape[2]
    side = sites // (TILE * COLS)
    pairs = side // 2
    part = width // GROUPS
    dma = pltpu.SemaphoreType.DMA
    outs = w_read.shape[1]
    operands = (
        syndrome, events, boundary, syn_table, event_table, bound_table, pos_table, norm_attn,
        w_query, w_key, w_value, w_out, norm_mlp, w_up, w_down, norm_final[None], w_read.T,
    )
    logits = pl.pallas_call(
        decoder,
        name="decoder",
        out_shape=jax.ShapeDtypeStruct((outs, 1, sites), F32),
        in_specs=[pl.BlockSpec(memory_space=pltpu.HBM)] * 17,
        out_specs=pl.BlockSpec(memory_space=pltpu.HBM),
        scratch_shapes=[
            *[pltpu.VMEM(a.shape, a.dtype) for a in operands],
            dma((11,)),
            dma((6, 2)),
            pltpu.VMEM((5, width, PAIR), F32),
            pltpu.VMEM((width, 4 * TILE), BF),
            pltpu.VMEM((TILE, PAIR), BF),
            pltpu.VMEM((2, width, width), BF),
            pltpu.VMEM((2, width, width), BF),
            pltpu.VMEM((2, width, width), BF),
            pltpu.VMEM((2, ff, width), BF),
            pltpu.VMEM((2, width, ff), BF),
            pltpu.VMEM((side, 16, PAIR), BF),
            pltpu.VMEM((side + 2, 16, PAIR), BF),
            pltpu.VMEM((4, pairs + 2, 2, width, PAIR), BF),
            pltpu.VMEM((pairs, width, 2 * WIDE), F32),
            pltpu.VMEM((pairs, width, 2 * WIDE), BF),
            pltpu.VMEM((side + 2, 3 * PAIR, width), BF),
            pltpu.VMEM((side + 2, GROUPS, part + ONES, 3 * PAIR), BF),
            pltpu.VMEM((pairs, width, 2 * WIDE), F32),
            pltpu.VMEM((pairs, width, 2 * WIDE), BF),
            pltpu.VMEM((pairs + 2, 2, 2, WIDE, width), BF),
            pltpu.VMEM((pairs + 2, 2, 2, GROUPS, part + ONES, WIDE), BF),
            pltpu.VMEM((side, outs, 1, WIDE), F32),
            dma((2, side)),
            dma((side + 2,)),
            dma((2, pairs)),
            dma((2, pairs)),
            dma((2,)),
            dma((2,)),
            dma((2, 2)),
            dma((2, 2)),
            dma((side,)),
            dma((side,)),
            dma,
        ],
        compiler_params=pltpu.CompilerParams(
            vmem_limit_bytes=56 * 1024 * 1024, collective_id=0, has_side_effects=True
        ),
    )(*operands)
    return logits


def solution(mesh):
    rows = P(("groups", "lx"), None)
    return jax.shard_map(
        on_device,
        mesh=mesh,
        in_specs=(rows,) * 3 + (P(),) * 14,
        out_specs=P(None, ("groups", "lx"), None),
        check_vma=False,
    )
```
